32 devices in a mesh: row: 4 (over z), col: 8 (over y, x, core).
Axes of the slice: x: 2, y: 2, z: 4, core: 2. Of those that a mesh axis runs over, the one named last changes fastest.
Arguments:
- gradient: bfloat16 [28672, 8192], P('row', 'col'), may hold values from -6 to 6
- projector: bfloat16 [8192, 1024], P('col', 'row'), may hold values from -0.0625 to 0.0625
- first_moment: float32 [1024, 28672], P('col', 'row'), may hold values from -2 to 2
- second_moment: float32 [1024, 28672], P('col', 'row'), may hold values from 0.0001 to 0.01
Outputs:
- update: float32 [28672, 8192], P('row', 'col')
- first_next: float32 [1024, 28672], P('col', 'row')
- second_next: float32 [1024, 28672], P('col', 'row')
The draws below stay inside these ranges and needn't reach their ends.
All inputs are finite; a program needn't handle non-finite values.
Results may differ from the reference program's by a relative error of at most 0.0058.
Values may be sent and summed in bfloat16 or wider, within the bound.
A program may use at most 128 MiB of HBM per device.

```python
import math
import jax
import jax.numpy as jnp

M = 28672
N = 8192
R = 1024


def levels(key, shape, shards, least, high):
    def one(position, parts):
        heights = jax.random.uniform(jax.random.fold_in(jax.random.fold_in(key, 6), position), (parts,), jnp.float32, least / len(shards), high / len(shards))
        return jnp.repeat(jnp.exp(heights), shape[position] // parts).reshape((-1,) + (1,) * (len(shape) - position - 1))

    loudness = one(*shards[0])
    for cut in shards[1:]:
        loudness = loudness * one(*cut)
    return loudness


def noise(own_key, extent, spread, reach, cuts=(), kind=jnp.bfloat16):
    drawn = spread * jax.random.normal(own_key, extent, jnp.float32)
    if cuts:
        drawn = drawn * levels(own_key, extent, cuts, -0.22, 0.18)
    return jnp.clip(drawn, -reach, reach).astype(kind)


def setup_inputs(seed: int = 0) -> dict:
    arg_keys = jax.random.split(jax.random.key(seed), 5)
    return {
        "gradient": noise(arg_keys[0], (M, N), 1.0, 6.0, ((0, 4), (1, 8))),
        "projector": noise(arg_keys[1], (N, R), N ** -0.5, 0.0625, ((0, 8), (1, 4))),
        "first_moment": noise(arg_keys[2], (R, M), 0.3, 2.0, ((0, 8), (1, 4)), jnp.float32),
        "second_moment": jnp.clip(jnp.exp(math.log(0.01) - 4.6051702 * jax.random.uniform(arg_keys[3], (R, M), jnp.float32) ** levels(arg_keys[3], (R, M), ((0, 8), (1, 4)), -0.2, 0.2)), 0.0001, 0.01),
    }


def reference(gradient, projector, first_moment, second_moment):
    compressed = jnp.dot(projector.T, gradient.T, preferred_element_type=jnp.float32)
    first_next = 0.9 * first_moment + 0.1 * compressed
    second_next = 0.999 * second_moment + 0.001 * compressed * compressed
    corr_first = 1.0 - 0.9 ** 10
    corr_second = 1.0 - 0.999 ** 10
    direction = (first_next / corr_first / (jnp.sqrt(second_next / corr_second) + 1e-08)).astype(jnp.bfloat16)
    update = jnp.dot(direction.T, projector.T, preferred_element_type=jnp.float32)
    return (update, first_next, second_next)
```

```python
import functools
import math

import jax
import jax.numpy as jnp
from jax import lax
from jax.experimental import pallas as pl
from jax.experimental.pallas import tpu as pltpu
from jax.sharding import PartitionSpec as P


SHARES = (1, 1, 1, 1)
BF16, F32 = jnp.bfloat16, jnp.float32


def swap(x, bit, n):
    return lax.ppermute(x, "col", [(i, i ^ (1 << bit)) for i in range(n)])


def shift(x, by, n):
    return lax.ppermute(x, "row", [(i, (i + by) % n) for i in range(n)])


def gather_rows(shard, n):
    if n == 1:
        return [shard]
    if n == 2:
        return [shard, shift(shard, 1, n)]
    found = {0: shard}
    up = down = shard
    for d in range(1, (n + 1) // 2):
        up, down = shift(up, 1, n), shift(down, -1, n)
        found[d], found[n - d] = up, down
    if n % 2 == 0:
        half = shard.shape[0] // 2
        found[n // 2] = jnp.concatenate([shift(up[:half], 1, n), shift(down[half:], -1, n)])
    return [found[d] for d in range(n)]


VMEM = pltpu.MemorySpace.VMEM


def pick_body(rows, parts, *refs):
    where, shards, outs, full = refs[0], refs[1 : parts + 1], refs[parts + 1 : -1], refs[-1]
    height = full.shape[0] // parts
    for d, shard in enumerate(shards):
        full[d * height : (d + 1) * height] = shard[...]
    for k, out in enumerate(outs):
        for p in range(out.shape[0] // rows):
            start = pl.multiple_of(where[k, p] * rows, rows)
            out[p * rows : (p + 1) * rows] = full[pl.ds(start, rows)]


def pick_blocks(found, where, rows):
    shape = (len(found) * found[0].shape[0], found[0].shape[1])
    turns = where.shape[0]
    return pl.pallas_call(
        functools.partial(pick_body, rows, len(found)),
        out_shape=[jax.ShapeDtypeStruct(shape, BF16)] * turns,
        in_specs=[pl.BlockSpec(memory_space=pltpu.MemorySpace.SMEM)]
        + [pl.BlockSpec(memory_space=VMEM)] * len(found),
        out_specs=[pl.BlockSpec(memory_space=VMEM)] * turns,
        scratch_shapes=[pltpu.VMEM(shape, BF16)],
        name="pick",
    )(where, *found)


def tile(*extents):
    return next(t for t in (1024, 896, 512, 256, 128) if math.gcd(*extents) % t == 0)


def cut(rows):
    unit = 512 if rows % (512 * sum(SHARES)) == 0 else 128
    edges = [0]
    for k in range(len(SHARES)):
        edges.append(rows * sum(SHARES[: k + 1]) // sum(SHARES) // unit * unit)
    return [(a, b - a) for a, b in zip(edges, edges[1:]) if b > a]


def adam_body(parts, *refs):
    terms, (first, second) = refs[:parts], refs[parts : parts + 2]
    direction, first_next, second_next = refs[-3:]
    c = terms[0][...].astype(F32)
    for t in terms[1:]:
        c = c + t[...].astype(F32)
    f = 0.9 * first[...] + 0.1 * c
    s = 0.999 * second[...] + 0.001 * c * c
    corr_first = 1.0 - 0.9**10
    corr_second = 1.0 - 0.999**10
    direction[...] = (f / corr_first / (jnp.sqrt(s / corr_second) + 1e-08)).astype(BF16)
    first_next[...] = f
    second_next[...] = s


def adam(offset, terms, first, second, moments):
    rows, cols = first.shape
    m = terms[0].shape[1]
    t = tile(m, offset)
    at = lambda i: (0, offset // t + i)
    last = lambda x: pl.BlockSpec((rows, t), functools.partial(lambda r, i: (r, i), x.shape[0] // rows - 1))
    whole = pl.BlockSpec((rows, t), at)
    anywhere = [pl.BlockSpec(memory_space=pl.ANY)] * len(moments)
    n = len(terms)
    return pl.pallas_call(
        functools.partial(adam_body, n),
        grid=(m // t,),
        out_shape=(
            jax.ShapeDtypeStruct((rows, m), BF16),
            jax.ShapeDtypeStruct((rows, cols), F32),
            jax.ShapeDtypeStruct((rows, cols), F32),
        ),
        in_specs=[last(x) for x in terms] + [whole, whole] + anywhere,
        out_specs=(pl.BlockSpec((rows, t), lambda i: (0, i)), whole, whole),
        input_output_aliases={n + 2: 1, n + 3: 2} if moments else {},
        cost_estimate=pl.CostEstimate(
            flops=20 * rows * m, bytes_accessed=rows * m * 24, transcendentals=2 * rows * m
        ),
        name="adam",
    )(*terms, first, second, *moments)


def back_body(parts, *refs):
    pieces, proj, out = refs[:parts], refs[parts], refs[-1]
    t = out.shape[0]
    at = pl.ds(pl.multiple_of(pl.program_id(0) * t, t), t)
    whole = jnp.concatenate([p[:, at] for p in pieces], axis=0)
    out[...] = lax.dot_general(whole, proj[...], (((0,), (0,)), ((), ())), preferred_element_type=F32)


def back(offset, pieces, proj, total, update):
    m = pieces[0].shape[1]
    ranks, width = proj.shape
    t = tile(m, offset)
    n = len(pieces)
    return pl.pallas_call(
        functools.partial(back_body, n),
        grid=(m // t,),
        out_shape=jax.ShapeDtypeStruct((total, width), F32),
        in_specs=[pl.BlockSpec(memory_space=VMEM)] * (n + 1)
        + [pl.BlockSpec(memory_space=pl.ANY)] * len(update),
        out_specs=pl.BlockSpec((t, width), lambda i: (offset // t + i, 0)),
        input_output_aliases={n + 1: 0} if update else {},
        cost_estimate=pl.CostEstimate(
            flops=2 * m * ranks * width, bytes_accessed=m * (2 * ranks + 4 * width), transcendentals=0
        ),
        name="back",
    )(*pieces, proj, *update)


def project(proj, grad):
    return lax.dot_general(proj, grad, (((1,), (1,)), ((), ())), preferred_element_type=F32)


def shards(n_row, n_col, gradient, projector, first_moment, second_moment):
    levels = n_col.bit_length() - 1
    own = first_moment.shape[0]
    ranks = own * n_col
    rows = gradient.shape[0]
    row, col = lax.axis_index("row"), lax.axis_index("col")

    found = gather_rows(projector.T, n_row)
    per_row = n_col // n_row
    orders, order = [], []
    for turn in range(2):
        bits = list(range(levels))
        if turn and levels > 1:
            bits = [0] + bits[:0:-1]
        away = []
        for p in range(n_col):
            digits = [(p >> (levels - 1 - k)) & 1 for k in range(levels)]
            away.append(sum((1 << b) for b, d in zip(bits, digits) if d == 0))
        owner = col ^ jnp.array(away, jnp.int32)
        order.append(lax.rem(row - owner // per_row + n_row, n_row) * per_row + owner % per_row)
        orders.append(bits)
    projs = list(pick_blocks(found, jnp.stack(order), own))

    update, moments = (), ()
    second = []
    for c, (offset, m) in enumerate(cut(rows)):
        bits, proj = orders[c % 2], projs[c % 2]
        if c == 2:
            proj, projs[1], *_ = lax.optimization_barrier((proj, projs[1], *second))
        grad = gradient[offset : offset + m]
        starts = [ranks - (ranks >> k) for k in range(levels + 1)]
        deep = min(2, levels)
        got = []
        rest = None
        for k in range(levels):
            a, b = starts[k], starts[k + 1]
            if k < deep:
                piece = project(proj[a:b], grad)
            else:
                if rest is None:
                    rest = project(proj[starts[deep] :], grad).astype(BF16)
                piece = rest[a - starts[deep] : b - starts[deep]].astype(F32)
            for j, r in enumerate(got):
                piece = piece + r[a - starts[j + 1] : b - starts[j + 1]].astype(F32)
            sent = piece.astype(BF16)
            if k == 1:
                second.append(sent)
            got.append(swap(sent, bits[k], n_col))
        if rest is None:
            rest = project(proj[starts[deep] :], grad)
        direction, *moments = adam(offset, [rest, *got], first_moment, second_moment, moments)
        held = [direction]
        for k in reversed(range(levels)):
            if k:
                whole = held[0] if len(held) == 1 else jnp.concatenate(held)
                held = [swap(whole, bits[k], n_col), whole]
            else:
                held = [swap(x, bits[k], n_col) for x in held] + held
        update = (back(offset, held, proj, rows, update),)
    return (update[0], *moments)


def solution(mesh):
    def step(*args):
        return shards(mesh.shape["row"], mesh.shape["col"], *args)

    return jax.shard_map(
        step,
        mesh=mesh,
        in_specs=(P("row", "col"), P("col", "row"), P("col", "row"), P("col", "row")),
        out_specs=(P("row", "col"), P("col", "row"), P("col", "row")),
        check_vma=False,
    )
```

```python
import functools
import math

import jax
import jax.numpy as jnp
from jax import lax
from jax.experimental import pallas as pl
from jax.experimental.pallas import tpu as pltpu
from jax.sharding import PartitionSpec as P


SHARES = (1, 1, 1, 1)
BF16, F32 = jnp.bfloat16, jnp.float32


def swap(x, bit, n):
    return lax.ppermute(x, "col", [(i, i ^ (1 << bit)) for i in range(n)])


def shift(x, by, n):
    return lax.ppermute(x, "row", [(i, (i + by) % n) for i in range(n)])


def gather_rows(shard, n):
    if n == 1:
        return [shard]
    if n == 2:
        return [shard, shift(shard, 1, n)]
    found = {0: shard}
    up = down = shard
    for d in range(1, (n + 1) // 2):
        up, down = shift(up, 1, n), shift(down, -1, n)
        found[d], found[n - d] = up, down
    if n % 2 == 0:
        half = shard.shape[0] // 2
        found[n // 2] = jnp.concatenate([shift(up[:half], 1, n), shift(down[half:], -1, n)])
    return [found[d] for d in range(n)]


VMEM = pltpu.MemorySpace.VMEM


def pick_body(rows, parts, *refs):
    where, shards, outs, full = refs[0], refs[1 : parts + 1], refs[parts + 1 : -1], refs[-1]
    height = full.shape[0] // parts
    for d, shard in enumerate(shards):
        full[d * height : (d + 1) * height] = shard[...]
    for k, out in enumerate(outs):
        for p in range(out.shape[0] // rows):
            start = pl.multiple_of(where[k, p] * rows, rows)
            out[p * rows : (p + 1) * rows] = full[pl.ds(start, rows)]


def pick_blocks(found, where, rows):
    shape = (len(found) * found[0].shape[0], found[0].shape[1])
    turns = where.shape[0]
    return pl.pallas_call(
        functools.partial(pick_body, rows, len(found)),
        out_shape=[jax.ShapeDtypeStruct(shape, BF16)] * turns,
        in_specs=[pl.BlockSpec(memory_space=pltpu.MemorySpace.SMEM)]
        + [pl.BlockSpec(memory_space=VMEM)] * len(found),
        out_specs=[pl.BlockSpec(memory_space=VMEM)] * turns,
        scratch_shapes=[pltpu.VMEM(shape, BF16)],
        name="pick",
    )(where, *found)


def tile(*extents):
    return next(t for t in (1024, 896, 512, 256, 128) if math.gcd(*extents) % t == 0)


def cut(rows):
    unit = 512 if rows % (512 * sum(SHARES)) == 0 else 128
    edges = [0]
    for k in range(len(SHARES)):
        edges.append(rows * sum(SHARES[: k + 1]) // sum(SHARES) // unit * unit)
    return [(a, b - a) for a, b in zip(edges, edges[1:]) if b > a]


def adam_body(parts, *refs):
    terms, (first, second) = refs[:parts], refs[parts : parts + 2]
    direction, first_next, second_next = refs[-3:]
    c = terms[0][...].astype(F32)
    for t in terms[1:]:
        c = c + t[...].astype(F32)
    f = 0.9 * first[...] + 0.1 * c
    s = 0.999 * second[...] + 0.001 * c * c
    corr_first = 1.0 - 0.9**10
    corr_second = 1.0 - 0.999**10
    direction[...] = (f / corr_first / (jnp.sqrt(s / corr_second) + 1e-08)).T.astype(BF16)
    first_next[...] = f
    second_next[...] = s


def adam(offset, terms, first, second, moments):
    rows, cols = first.shape
    m = terms[0].shape[1]
    t = tile(m, offset)
    at = lambda i: (0, offset // t + i)
    last = lambda x: pl.BlockSpec((rows, t), functools.partial(lambda r, i: (r, i), x.shape[0] // rows - 1))
    whole = pl.BlockSpec((rows, t), at)
    anywhere = [pl.BlockSpec(memory_space=pl.ANY)] * len(moments)
    n = len(terms)
    return pl.pallas_call(
        functools.partial(adam_body, n),
        grid=(m // t,),
        out_shape=(
            jax.ShapeDtypeStruct((m, rows), BF16),
            jax.ShapeDtypeStruct((rows, cols), F32),
            jax.ShapeDtypeStruct((rows, cols), F32),
        ),
        in_specs=[last(x) for x in terms] + [whole, whole] + anywhere,
        out_specs=(pl.BlockSpec((t, rows), lambda i: (i, 0)), whole, whole),
        input_output_aliases={n + 2: 1, n + 3: 2} if moments else {},
        cost_estimate=pl.CostEstimate(
            flops=20 * rows * m, bytes_accessed=rows * m * 24, transcendentals=2 * rows * m
        ),
        name="adam",
    )(*terms, first, second, *moments)


def back_body(parts, *refs):
    pieces, proj, out = refs[:parts], refs[parts], refs[-1]
    t = out.shape[0]
    at = pl.ds(pl.multiple_of(pl.program_id(0) * t, t), t)
    whole = jnp.concatenate([p[at] for p in pieces], axis=1)
    out[...] = jnp.dot(whole, proj[...], preferred_element_type=F32)


def back(offset, pieces, proj, total, update):
    m = pieces[0].shape[0]
    ranks, width = proj.shape
    t = tile(m, offset)
    n = len(pieces)
    return pl.pallas_call(
        functools.partial(back_body, n),
        grid=(m // t,),
        out_shape=jax.ShapeDtypeStruct((total, width), F32),
        in_specs=[pl.BlockSpec(memory_space=VMEM)] * (n + 1)
        + [pl.BlockSpec(memory_space=pl.ANY)] * len(update),
        out_specs=pl.BlockSpec((t, width), lambda i: (offset // t + i, 0)),
        input_output_aliases={n + 1: 0} if update else {},
        cost_estimate=pl.CostEstimate(
            flops=2 * m * ranks * width, bytes_accessed=m * (2 * ranks + 4 * width), transcendentals=0
        ),
        name="back",
    )(*pieces, proj, *update)


def project(proj, grad):
    return lax.dot_general(proj, grad, (((1,), (1,)), ((), ())), preferred_element_type=F32)


def shards(n_row, n_col, gradient, projector, first_moment, second_moment):
    levels = n_col.bit_length() - 1
    own = first_moment.shape[0]
    ranks = own * n_col
    rows = gradient.shape[0]
    row, col = lax.axis_index("row"), lax.axis_index("col")

    found = gather_rows(projector.T, n_row)
    per_row = n_col // n_row
    orders, order = [], []
    for turn in range(2):
        bits = list(range(levels))
        if turn and levels > 1:
            bits = [0] + bits[:0:-1]
        away = []
        for p in range(n_col):
            digits = [(p >> (levels - 1 - k)) & 1 for k in range(levels)]
            away.append(sum((1 << b) for b, d in zip(bits, digits) if d == 0))
        owner = col ^ jnp.array(away, jnp.int32)
        order.append(lax.rem(row - owner // per_row + n_row, n_row) * per_row + owner % per_row)
        orders.append(bits)
    projs = list(pick_blocks(found, jnp.stack(order), own))

    update, moments = (), ()
    second = []
    for c, (offset, m) in enumerate(cut(rows)):
        bits, proj = orders[c % 2], projs[c % 2]
        if c == 2:
            proj, projs[1], *_ = lax.optimization_barrier((proj, projs[1], *second))
        grad = gradient[offset : offset + m]
        starts = [ranks - (ranks >> k) for k in range(levels + 1)]
        deep = min(2, levels)
        got = []
        rest = None
        for k in range(levels):
            a, b = starts[k], starts[k + 1]
            if k < deep:
                piece = project(proj[a:b], grad)
            else:
                if rest is None:
                    rest = project(proj[starts[deep] :], grad).astype(BF16)
                piece = rest[a - starts[deep] : b - starts[deep]].astype(F32)
            for j, r in enumerate(got):
                piece = piece + r[a - starts[j + 1] : b - starts[j + 1]].astype(F32)
            sent = piece.astype(BF16)
            if k == 1:
                second.append(sent)
            got.append(swap(sent, bits[k], n_col))
        if rest is None:
            rest = project(proj[starts[deep] :], grad)
        direction, *moments = adam(offset, [rest, *got], first_moment, second_moment, moments)
        held = [direction]
        for k in reversed(range(levels)):
            if k:
                whole = held[0] if len(held) == 1 else jnp.concatenate(held, axis=1)
                held = [swap(whole, bits[k], n_col), whole]
            else:
                held = [swap(x, bits[k], n_col) for x in held] + held
        update = (back(offset, held, proj, rows, update),)
    return (update[0], *moments)


def solution(mesh):
    def step(*args):
        return shards(mesh.shape["row"], mesh.shape["col"], *args)

    return jax.shard_map(
        step,
        mesh=mesh,
        in_specs=(P("row", "col"), P("col", "row"), P("col", "row"), P("col", "row")),
        out_specs=(P("row", "col"), P("col", "row"), P("col", "row")),
        check_vma=False,
    )
```
